512 devices in a mesh: dp: 16 (over y, core), tensor: 32 (over x, z).
Axes of the slice: x: 4, y: 8, z: 8, core: 2. Of those that a mesh axis runs over, the one named last changes fastest.
Arguments:
- hidden_in: bfloat16 [16, 32, 128, 2, 4096], P('dp', None, None, None, 'tensor'), may hold values from -6 to 6
- conv_weight: bfloat16 [3, 3, 2, 4096], P(None, None, None, 'tensor'), may hold values from -2 to 2
- proj_weight: bfloat16 [4096, 2048], P('tensor'), may hold values from -0.125 to 0.125
- out_grad: bfloat16 [16, 32, 128, 2048], P('dp', 'tensor'), may hold values from -6 to 6
- sample_gate: float32 [16, 2048], P('dp'), may hold values from -4 to 4
Outputs:
- hidden_grad: bfloat16 [16, 32, 128, 2, 4096], P('dp', None, None, None, 'tensor')
- proj_grad: bfloat16 [4096, 2048], P('tensor')
- conv_grad: float32 [3, 3, 2, 4096], P(None, None, None, 'tensor')
The draws below stay inside these ranges and needn't reach their ends.
All inputs are finite; a program needn't handle non-finite values.
Results may differ from the reference program's by a relative error of at most 0.0057.
Values may be sent and summed in bfloat16 or wider, within the bound.
A program may use at most 128 MiB of HBM per device.

```python
import math
import jax
import jax.numpy as jnp
from jax import lax

D = 2048
HID = 4096
IMG_W = 128
IMG_H = 32
SAMPLES = 16


def block_levels(stream_key, dims, cuts, least, top_value):
    level, own = 1.0, jax.random.fold_in(stream_key, 6)
    for position, blocks in cuts:
        heights = jnp.exp(jax.random.uniform(jax.random.fold_in(own, position), (blocks,), jnp.float32, least / len(cuts), top_value / len(cuts)))
        level = level * jnp.repeat(heights, dims[position] // blocks).reshape([-1 if axis == position else 1 for axis in range(len(dims))])
    return level


def gaussian(key, dims, scale, bound, cuts=(), dtype=jnp.bfloat16):
    result = jax.random.normal(key, dims, jnp.float32) * scale
    if len(cuts) > 0:
        result = block_levels(key, dims, cuts, -0.22, 0.18) * result
    return jnp.clip(result, min=-bound, max=bound).astype(dtype)


def setup_inputs(seed: int = 0) -> dict:
    arg_keys = jax.random.split(jax.random.key(seed), 6)
    return {
        "hidden_in": gaussian(arg_keys[0], (SAMPLES, IMG_H, IMG_W, 2, HID), 1.0, 6.0, ((0, 16), (4, 32))),
        "conv_weight": gaussian(arg_keys[1], (3, 3, 2, HID), 9 ** -0.5, 2.0, ((3, 32),)),
        "proj_weight": gaussian(arg_keys[2], (HID, D), D ** -0.5, 0.125, ((0, 32),)),
        "out_grad": gaussian(arg_keys[3], (SAMPLES, IMG_H, IMG_W, D), 1.0, 6.0, ((0, 16), (1, 32))),
        "sample_gate": gaussian(arg_keys[4], (SAMPLES, D), 1.0, 4.0, ((0, 16),), jnp.float32),
    }


def depthwise(volume, kernel, mirror):
    height = volume.shape[1]
    across = volume.shape[2]
    padded = jnp.pad(volume, ((0, 0), (1, 1), (1, 1), (0, 0), (0, 0)))
    summed = jnp.zeros(volume.shape, jnp.float32)
    for i in range(3):
        for j in range(3):
            a = 2 - i if mirror else i
            b = 2 - j if mirror else j
            summed = summed + kernel[i, j].astype(jnp.float32) * padded[:, a:a + height, b:b + across]
    return summed

def kernel_terms(grad_pre, volume):
    height = volume.shape[1]
    across = volume.shape[2]
    padded = jnp.pad(volume, ((0, 0), (1, 1), (1, 1), (0, 0), (0, 0)))
    rows_out = []
    for i in range(3):
        row_terms = []
        for j in range(3):
            row_terms.append(lax.optimization_barrier(jnp.sum(grad_pre * padded[:, i:i + height, j:j + across], axis=(0, 1, 2))))
        rows_out.append(jnp.stack(row_terms))
    return jnp.stack(rows_out)

def reference(hidden_in, conv_weight, proj_weight, out_grad, sample_gate):
    grad_scale = 1.0 / math.sqrt(SAMPLES * IMG_H * IMG_W)

    def per_sample(running, inputs):
        volume, grad_rows, gate_rows = inputs
        volume = volume[None]
        gated_grad = (grad_rows.astype(jnp.float32) * gate_rows).astype(jnp.bfloat16)
        conv_out = depthwise(volume, conv_weight, False)
        value_part = conv_out[..., 0, :]
        gate_part = conv_out[..., 1, :]
        gate_sig = jax.nn.sigmoid(gate_part)
        mixed_act = (value_part * gate_part * gate_sig).astype(jnp.bfloat16)
        flat_grad = gated_grad.reshape(-1, D)
        flat_act = mixed_act.reshape(-1, HID)
        grad_mixed = jnp.dot(flat_grad, proj_weight.T, preferred_element_type=jnp.float32).reshape(mixed_act.shape)
        proj_sum = running[0] + jnp.dot(flat_act.T, flat_grad, preferred_element_type=jnp.float32)
        grad_pre = jnp.stack([grad_mixed * gate_part * gate_sig, grad_mixed * value_part * gate_sig * (1.0 + gate_part * (1.0 - gate_sig))], axis=-2)
        hidden_grad = depthwise(grad_pre, conv_weight, True).astype(jnp.bfloat16)
        kernel_sum = running[1] + kernel_terms(grad_pre, volume)
        return ((proj_sum, kernel_sum), hidden_grad[0])
    start_state = (jnp.zeros((HID, D), jnp.float32), jnp.zeros((3, 3, 2, HID), jnp.float32))
    sums, hidden_grad = lax.scan(per_sample, start_state, (hidden_in, out_grad, sample_gate))
    proj_grad = (sums[0] * grad_scale).astype(jnp.bfloat16)
    conv_grad = sums[1] * grad_scale
    return (hidden_grad, proj_grad, conv_grad)
```

```python
import math

import jax
import jax.numpy as jnp
from jax import lax
from jax.experimental import pallas as pl
from jax.experimental.pallas import tpu as pltpu
from jax.sharding import PartitionSpec as P

NX, NZ, NY = 4, 8, 8
H, W, C = 32, 128, 128
QN, QD = 4, 512
F32, BF16 = jnp.float32, jnp.bfloat16


def down(t):
    rolled = pltpu.roll(t, 2, 0)
    return jnp.where(lax.broadcasted_iota(jnp.int32, t.shape, 0) >= 2, rolled, 0.0)


def up(t):
    n = t.shape[0]
    rolled = pltpu.roll(t, n - 2, 0)
    return jnp.where(lax.broadcasted_iota(jnp.int32, t.shape, 0) < n - 2, rolled, 0.0)


def taps(rows, wpat, j, mirror):
    total = None
    for i in range(3):
        w = wpat[(2 - i if mirror else i) * 3 + j]
        term = rows[i].reshape(2 * W // 8, 8, C) * w[None]
        total = term if total is None else total + term
    return total.reshape(2 * W, C)


def kernel(grad_scale, hid_ref, cw_ref, pw_ref, og_ref, sg_ref, hout_ref, proj_ref, cg_ref,
           hpad, wpat, cs, fv, fg, mown, mix, mix_t, g, w_all, gms, gmr, gp, ho,
           pacc, p1s, p1r, r2s, r2r, r3s, r3r, pfin, cpart, cr1, cr2,
           hid_sem, out_sem, pf_sem, ring_s, ring_r, ws_s, ws_r, wf_s, wf_r, mx_s, mx_r, gm_s, gm_r,
           p1_s, p1_rs, r2_s, r2_rs, r3_s, r3_rs, r4_s, r4_rs, pf_s, pf_r, c1_s, c1_r, c2_s, c2_r):
    dp = lax.axis_index("dp")
    tensor = lax.axis_index("tensor")
    my, core = dp // 2, lax.rem(dp, 2)
    mx, mz = tensor // NZ, lax.rem(tensor, NZ)

    def at_z(d):
        return (dp, mx * NZ + lax.rem(mz + d + NZ, NZ))

    def at_x(j):
        return (dp, lax.rem(mx + j, NX) * NZ + mz)

    def at_y(j):
        return (lax.rem(my + j, NY) * 2 + core, tensor)

    partner = (my * 2 + 1 - core, tensor)
    sends = []

    def send(src, dst, ssem, rsem, to):
        copy = pltpu.make_async_remote_copy(
            src_ref=src, dst_ref=dst, send_sem=ssem, recv_sem=rsem,
            device_id=to, device_id_type=pl.DeviceIdType.MESH)
        copy.start()
        sends.append(copy)

    def arrived(ref, rsem):
        pltpu.make_async_copy(ref, ref, rsem).wait()

    barrier = pltpu.get_barrier_semaphore()
    friends = [at_z(1), at_z(-1), partner] + [at_x(j) for j in range(1, NX)] + [at_y(j) for j in range(1, NY)]
    for to in friends:
        pl.semaphore_signal(barrier, inc=1, device_id=to, device_id_type=pl.DeviceIdType.MESH)
    hid_copy = pltpu.make_async_copy(hid_ref, hpad.at[pl.ds(1, H)], hid_sem)
    hid_copy.start()
    own_w = pltpu.make_async_copy(pw_ref, w_all.at[0], pf_sem)
    own_w.start()
    for q in range(QN):
        cols = slice(q * QD, (q + 1) * QD)
        g[q, 0] = (og_ref[:, cols].astype(F32) * sg_ref[:, cols]).astype(BF16)
    hpad[0] = jnp.zeros((2 * W, C), BF16)
    hpad[H + 1] = jnp.zeros((2 * W, C), BF16)
    gp[0] = jnp.zeros((2 * W, C), F32)
    gp[H + 1] = jnp.zeros((2 * W, C), F32)
    even = lax.rem(lax.broadcasted_iota(jnp.int32, (8, C), 0), 2) == 0
    for i in range(3):
        for j in range(3):
            pair = cw_ref[i, j].astype(F32)
            wpat[i * 3 + j] = jnp.where(
                even, jnp.broadcast_to(pair[0:1], (8, C)), jnp.broadcast_to(pair[1:2], (8, C)))
    pl.semaphore_wait(barrier, len(friends))

    def ring(q, step, d):
        src = step - 1 if d == 0 else (NZ - step + 1) % NZ
        dst = step if d == 0 else NZ - step
        send(g.at[q, src], g.at[q, dst], ring_s.at[d, step - 1, q], ring_r.at[d, step - 1, q],
             at_z(1 if d == 0 else -1))

    def ring_here(q, step, d):
        dst = step if d == 0 else NZ - step
        arrived(g.at[q, dst], ring_r.at[d, step - 1, q])

    def carries(q, step, d):
        return step < 4 or q % 2 == d

    def forward(q, step):
        for d in range(2):
            ring_here(q, step - 1, d)
            if carries(q, step, d):
                ring(q, step, d)

    for q in range(QN):
        for d in range(2):
            ring(q, 1, d)
    half = pl.ds(pl.multiple_of(core * (C // 2), C // 2), C // 2)
    other = pl.ds(pl.multiple_of((1 - core) * (C // 2), C // 2), C // 2)
    for j in (2, 1, 3):
        send(pw_ref.at[half], w_all.at[NX - j, half], ws_s.at[j - 1], ws_r.at[NX - j - 1], at_x(j))

    hid_copy.wait()

    def activate(j):
        x_of = lax.rem(mx + j, NX)

        def body(slot, _):
            r = x_of * NZ + lax.rem(mz - slot + NZ, NZ)
            rows = [hpad[r + i].astype(F32) for i in range(3)]
            out = taps(rows, wpat, 1, False) + down(taps(rows, wpat, 0, False)) + up(taps(rows, wpat, 2, False))
            cs[...] = out
            value = cs[pl.ds(0, W, stride=2), :]
            gate = cs[pl.ds(1, W, stride=2), :]
            sig = 1.0 / (1.0 + jnp.exp(-gate))
            a = gate * sig
            fv[r] = a
            fg[r] = value * sig * (1.0 + gate * (1.0 - sig))
            act = (value * a).astype(BF16)
            if j == 0:
                mix[0, slot] = act
            else:
                mown[j - 1, slot] = act
            return 0

        lax.fori_loop(0, NZ, body, 0)

    def send_mixed(j):
        send(mown.at[j - 1], mix.at[NX - j], mx_s.at[j - 1], mx_r.at[NX - j - 1], at_x(j))

    activate(2)
    send_mixed(2)
    activate(1)
    send_mixed(1)
    forward(0, 2)
    forward(1, 2)
    activate(3)
    send_mixed(3)
    activate(0)
    for j in (1, 3, 2):
        arrived(w_all.at[j, half], ws_r.at[j - 1])
        send(w_all.at[j, half], w_all.at[j, half], wf_s.at[j - 1], wf_r.at[j - 1], partner)
    forward(0, 3)
    forward(1, 3)

    def transposed(j):
        mix_t[j * C:(j + 1) * C, :] = mix[j].reshape(NZ * W, C).T

    transposed(0)
    for d in range(2):
        ring_here(d, 3, 1 - d)
    forward_q = [0, 1]
    for q in forward_q:
        ring_here(q, 3, q % 2)
        ring(q, 4, q % 2)
    for q in (2, 3):
        forward(q, 2)
    for j in (1, 3, 2):
        arrived(mix.at[j], mx_r.at[j - 1])
        transposed(j)
    own_w.wait()
    for j in (1, 3, 2):
        arrived(w_all.at[j, other], wf_r.at[j - 1])

    def row_of(x_of, slot):
        return x_of * NZ + lax.rem(mz - slot + NZ, NZ)

    def grad_rows(slots):
        total = None
        for q in range(QN):
            left = jnp.concatenate([g[q, s] for s in slots], axis=0)
            right = w_all[:, :, q * QD:(q + 1) * QD].reshape(NX * C, QD)
            part = lax.dot_general(left, right, (((1,), (1,)), ((), ())), preferred_element_type=F32)
            total = part if total is None else total + part
        for n, s in enumerate(slots):
            rows = total[n * W:(n + 1) * W].astype(BF16)
            gmr[row_of(mx, s)] = rows[:, :C]
            for j in range(1, NX):
                gms[j - 1, s] = rows[:, j * C:(j + 1) * C]
        for s in slots:
            for j in (2, 1, 3):
                send(gms.at[j - 1, s], gmr.at[row_of(mx, s)], gm_s.at[j - 1, s], gm_r.at[j - 1, s], at_x(j))

    def grad_pre(slots):
        for s in slots:
            for j in range(NX):
                r = row_of(lax.rem(mx - j + NX, NX), s)
                if j > 0:
                    arrived(gmr.at[r], gm_r.at[j - 1, s])
                gm = gmr[r].astype(F32)
                gp[r + 1, pl.ds(0, W, stride=2), :] = gm * fv[r]
                gp[r + 1, pl.ds(1, W, stride=2), :] = gm * fg[r]

    def proj_pair(u):
        p1 = jnp.dot(mix_t[...], g[2 * u + 1 - core].reshape(NZ * W, QD), preferred_element_type=F32)
        p1s[u] = p1.astype(BF16)
        send(p1s.at[u], p1r.at[u], p1_s.at[u], p1_rs.at[u], partner)
        pacc[u] = jnp.dot(mix_t[...], g[2 * u + core].reshape(NZ * W, QD), preferred_element_type=F32)

    def over_x(u):
        arrived(p1r.at[u], p1_rs.at[u])
        for j in (2, 1, 3, 0):
            rows = slice(j * C, (j + 1) * C)
            s1 = pacc[u, rows] + p1r[u, rows].astype(F32)
            if j == 0:
                pacc[u, rows] = s1
            else:
                r2s[u, j - 1] = s1.astype(BF16)
                send(r2s.at[u, j - 1], r2r.at[u, NX - j - 1], r2_s.at[u, j - 1], r2_rs.at[u, NX - j - 1], at_x(j))

    def over_y(u):
        for j in (1, 3, 2):
            arrived(r2r.at[u, j - 1], r2_rs.at[u, j - 1])
        s2 = pacc[u, 0:C]
        for j in range(NX - 1):
            s2 = s2 + r2r[u, j].astype(F32)
        pacc[u, 0:C] = s2
        r3s[u] = s2.astype(BF16).reshape(NY, C // NY, QD)
        for j in (4, 3, 5, 2, 6, 1, 7):
            send(r3s.at[u, lax.rem(my + j, NY)], r3r.at[u, j - 1], r3_s.at[u, j - 1], r3_rs.at[u, j - 1], at_y(j))

    def spread(u):
        piece = pl.ds(pl.multiple_of(my * (C // NY), C // NY), C // NY)
        s3 = pacc[u, piece]
        for j in range(1, NY):
            arrived(r3r.at[u, j - 1], r3_rs.at[u, j - 1])
            s3 = s3 + r3r[u, j - 1].astype(F32)
        pfin[2 * u + core, my] = (s3 * grad_scale).astype(BF16)
        for j in (4, 3, 5, 2, 6, 1, 7):
            send(pfin.at[2 * u + core, my], pfin.at[2 * u + core, my], r4_s.at[u, j - 1], r4_rs.at[u, j - 1], at_y(j))

    def hand_over(u):
        for j in range(1, NY):
            arrived(pfin.at[2 * u + core, lax.rem(my - j + NY, NY)], r4_rs.at[u, j - 1])
        send(pfin.at[2 * u + core], pfin.at[2 * u + core], pf_s.at[u], pf_r.at[u], partner)

    for q in (0, 1):
        ring_here(q, 4, q % 2)
    proj_pair(0)
    for q in (2, 3):
        forward(q, 3)
    grad_rows((0, 1))
    grad_rows((7,))
    over_x(0)
    for q in (2, 3):
        ring_here(q, 3, q % 2)
        ring(q, 4, q % 2)
    grad_rows((2, 6))
    for q in (2, 3):
        ring_here(q, 3, 1 - q % 2)
    grad_rows((3, 5))
    over_y(0)
    for q in (2, 3):
        ring_here(q, 4, q % 2)
    grad_rows((4,))
    proj_pair(1)
    grad_pre((0, 1, 7))
    over_x(1)
    spread(0)
    grad_pre((2, 6, 3, 5, 4))

    def back(r, sums):
        rows = [gp[r + i] for i in range(3)]
        hid = [hpad[r + i].astype(F32) for i in range(3)]
        out = taps(rows, wpat, 1, True) + up(taps(rows, wpat, 0, True)) + down(taps(rows, wpat, 2, True))
        ho[r] = out.astype(BF16)
        moved = (up(rows[1]), rows[1], down(rows[1]))
        new = []
        for i in range(3):
            for j in range(3):
                prod = (moved[j] * hid[i]).reshape(2 * W // 8, 8, C)
                new.append(sums[i * 3 + j] + jnp.sum(prod, axis=0))
        return tuple(new)

    group = H // 4
    outs = []
    sums = tuple(jnp.zeros((8, C), F32) for _ in range(9))
    for n in range(4):
        sums = lax.fori_loop(n * group, (n + 1) * group, back, sums)
        copy = pltpu.make_async_copy(ho.at[pl.ds(n * group, group)], hout_ref.at[pl.ds(n * group, group)], out_sem.at[n])
        copy.start()
        outs.append(copy)
        if n == 0:
            over_y(1)
        if n == 1:
            hand_over(0)
        if n == 2:
            spread(1)
    for t in range(9):
        cpart[t] = sums[t]
    send(cpart, cr1, c1_s, c1_r, partner)
    arrived(cr1, c1_r)
    both = cpart[...] + cr1[...]
    cr2[my] = both
    for j in (4, 3, 5, 2, 6, 1, 7):
        send(cr2.at[my], cr2.at[my], c2_s.at[j - 1], c2_r.at[j - 1], at_y(j))
    hand_over(1)
    for j in range(1, NY):
        arrived(cr2.at[lax.rem(my - j + NY, NY)], c2_r.at[j - 1])
    total = cr2[0]
    for y in range(1, NY):
        total = total + cr2[y]
    for i in range(3):
        for j in range(3):
            t = total[i * 3 + j]
            t = (t[0:2] + t[2:4]) + (t[4:6] + t[6:8])
            cg_ref[i, j] = t * grad_scale
    for u in range(2):
        mine = 2 * u + core
        arrived(pfin.at[2 * u + 1 - core], pf_r.at[u])
    for q in range(QN):
        proj_ref[:, q * QD:(q + 1) * QD] = pfin[q].reshape(C, QD)
    for copy in outs:
        copy.wait()
    for copy in sends:
        copy.wait_send()


def on_device(hidden_in, conv_weight, proj_weight, out_grad, sample_gate):
    grad_scale = 1.0 / math.sqrt(lax.axis_size("dp") * H * W)
    vmem = pl.BlockSpec(memory_space=pltpu.VMEM)
    hbm = pl.BlockSpec(memory_space=pl.ANY)
    dma = pltpu.SemaphoreType.DMA
    d = proj_weight.shape[1]
    hout, proj, conv = pl.pallas_call(
        lambda *refs: kernel(grad_scale, *refs),
        name="mixffn_backward",
        out_shape=(
            jax.ShapeDtypeStruct((H, 2 * W, C), BF16),
            jax.ShapeDtypeStruct((C, d), BF16),
            jax.ShapeDtypeStruct((3, 3, 2, C), F32),
        ),
        in_specs=[hbm, vmem, vmem, vmem, vmem],
        out_specs=(hbm, vmem, vmem),
        scratch_shapes=[
            pltpu.VMEM((H + 2, 2 * W, C), BF16),
            pltpu.VMEM((9, 8, C), F32),
            pltpu.VMEM((2 * W, C), F32),
            pltpu.VMEM((H, W, C), F32),
            pltpu.VMEM((H, W, C), F32),
            pltpu.VMEM((NX - 1, NZ, W, C), BF16),
            pltpu.VMEM((NX, NZ, W, C), BF16),
            pltpu.VMEM((NX * C, NZ * W), BF16),
            pltpu.VMEM((QN, NZ, W, QD), BF16),
            pltpu.VMEM((NX, C, d), BF16),
            pltpu.VMEM((NX - 1, NZ, W, C), BF16),
            pltpu.VMEM((H, W, C), BF16),
            pltpu.VMEM((H + 2, 2 * W, C), F32),
            pltpu.VMEM((H, 2 * W, C), BF16),
            pltpu.VMEM((2, NX * C, QD), F32),
            pltpu.VMEM((2, NX * C, QD), BF16),
            pltpu.VMEM((2, NX * C, QD), BF16),
            pltpu.VMEM((2, NX - 1, C, QD), BF16),
            pltpu.VMEM((2, NX - 1, C, QD), BF16),
            pltpu.VMEM((2, NY, C // NY, QD), BF16),
            pltpu.VMEM((2, NY - 1, C // NY, QD), BF16),
            pltpu.VMEM((QN, NY, C // NY, QD), BF16),
            pltpu.VMEM((9, 8, C), F32),
            pltpu.VMEM((9, 8, C), F32),
            pltpu.VMEM((NY, 9, 8, C), F32),
            dma, dma((4,)), dma,
            dma((2, 4, QN)), dma((2, 4, QN)),
            dma((3,)), dma((3,)), dma((3,)), dma((3,)), dma((3,)), dma((3,)),
            dma((3, NZ)), dma((3, NZ)),
            dma((2,)), dma((2,)), dma((2, 3)), dma((2, 3)),
            dma((2, 7)), dma((2, 7)), dma((2, 7)), dma((2, 7)),
            dma((2,)), dma((2,)),
            dma, dma, dma((7,)), dma((7,)),
        ],
        compiler_params=pltpu.CompilerParams(
            collective_id=0, has_side_effects=True, vmem_limit_bytes=60000 * 1024),
    )(
        hidden_in.reshape(H, 2 * W, C),
        conv_weight,
        proj_weight,
        out_grad.reshape(W, d),
        sample_gate,
    )
    return hout.reshape(hidden_in.shape), proj, conv


def solution(mesh):
    in_specs = (
        P("dp", None, None, None, "tensor"),
        P(None, None, None, "tensor"),
        P("tensor", None),
        P("dp", "tensor", None, None),
        P("dp", None),
    )
    out_specs = (
        P("dp", None, None, None, "tensor"),
        P("tensor", None),
        P(None, None, None, "tensor"),
    )
    return jax.shard_map(
        on_device, mesh=mesh, in_specs=in_specs, out_specs=out_specs, check_vma=False
    )
```

```python
import math

import jax
import jax.numpy as jnp
from jax import lax
from jax.experimental import pallas as pl
from jax.experimental.pallas import tpu as pltpu
from jax.sharding import PartitionSpec as P

NX, NZ, NY = 4, 8, 8
H, W, C = 32, 128, 128
QN, QD = 8, 256
F32, BF16 = jnp.float32, jnp.bfloat16


def down(t):
    rolled = pltpu.roll(t, 2, 0)
    return jnp.where(lax.broadcasted_iota(jnp.int32, t.shape, 0) >= 2, rolled, 0.0)


def up(t):
    n = t.shape[0]
    rolled = pltpu.roll(t, n - 2, 0)
    return jnp.where(lax.broadcasted_iota(jnp.int32, t.shape, 0) < n - 2, rolled, 0.0)


def taps(rows, wpat, j, mirror):
    total = None
    for i in range(3):
        w = wpat[(2 - i if mirror else i) * 3 + j]
        term = rows[i].reshape(2 * W // 8, 8, C) * w[None]
        total = term if total is None else total + term
    return total.reshape(2 * W, C)


def kernel(grad_scale, hid_ref, cw_ref, pw_ref, og_ref, sg_ref, hout_ref, proj_ref, cg_ref,
           og, cw, sg, hpad, wpat, cs, fv, fg, mown, mix, mix_t, g, w_all, gms, gmr, gp, ho,
           pacc, p1f, p1s, p1r, r2s, r2r, r3s, r3r, ys, yr, xs, xr, pfin, cpart, cs18, cr1, cr2, cg,
           in_sem, out_sem, po_sem, ring_s, ring_r, ws_s, ws_r, wf_s, wf_r, mx_s, mx_r, gm_s, gm_r,
           p1_s, p1_rs, r2_s, r2_rs, r3_s, r3_rs, ys_s, ys_r, xs_s, xs_r, r4_s, r4_rs, pf_s, pf_r, c1_s, c1_r, c2_s, c2_r):
    dp = lax.axis_index("dp")
    tensor = lax.axis_index("tensor")
    my, core = dp // 2, lax.rem(dp, 2)
    mx, mz = tensor // NZ, lax.rem(tensor, NZ)
    far_first = (4, 3, 5, 2, 6, 1, 7)

    def at_z(d):
        return (dp, mx * NZ + lax.rem(mz + d + NZ, NZ))

    def at_x(j):
        return (dp, lax.rem(mx + j, NX) * NZ + mz)

    def at_y(j):
        return (lax.rem(my + j, NY) * 2 + core, tensor)

    partner = (my * 2 + 1 - core, tensor)

    def send(src, dst, ssem, rsem, to):
        copy = pltpu.make_async_remote_copy(
            src_ref=src, dst_ref=dst, send_sem=ssem, recv_sem=rsem,
            device_id=to, device_id_type=pl.DeviceIdType.MESH)
        copy.start()

    def local(src, dst, sem):
        copy = pltpu.make_async_copy(src, dst, sem)
        copy.start()
        return copy

    def arrived(ref, rsem):
        pltpu.make_async_copy(ref, ref, rsem).wait()

    barrier = pltpu.get_barrier_semaphore()
    friends = [at_z(1), at_z(-1), partner] + [at_x(j) for j in range(1, NX)] + [at_y(j) for j in range(1, NY)]
    for to in friends:
        pl.semaphore_signal(barrier, inc=1, device_id=to, device_id_type=pl.DeviceIdType.MESH)
    og_in = local(og_ref, og, in_sem.at[0])
    sg_in = local(sg_ref, sg, in_sem.at[4])
    cw_in = local(cw_ref, cw, in_sem.at[5])
    w_in = local(pw_ref, w_all.at[0], in_sem.at[1])
    hid_in = local(hid_ref, hpad.at[pl.ds(1, H)], in_sem.at[2])
    hpad[0] = jnp.zeros((2 * W, C), BF16)
    hpad[H + 1] = jnp.zeros((2 * W, C), BF16)
    gp[0] = jnp.zeros((2 * W, C), F32)
    gp[H + 1] = jnp.zeros((2 * W, C), F32)
    cs18[...] = jnp.zeros(cs18.shape, F32)
    cpart[...] = jnp.zeros(cpart.shape, F32)
    cw_in.wait()
    even = lax.rem(lax.broadcasted_iota(jnp.int32, (8, C), 0), 2) == 0
    for i in range(3):
        for j in range(3):
            pair = cw[i, j].astype(F32)
            wpat[i * 3 + j] = jnp.where(
                even, jnp.broadcast_to(pair[0:1], (8, C)), jnp.broadcast_to(pair[1:2], (8, C)))
    og_in.wait()
    sg_in.wait()
    for q in range(QN):
        cols = slice(q * QD, (q + 1) * QD)
        g[q, 0] = (og[:, cols].astype(F32) * sg[:, cols]).astype(BF16)
    w_in.wait()
    pl.semaphore_wait(barrier, len(friends))

    def ring(q, step, d):
        src = step - 1 if d == 0 else (NZ - step + 1) % NZ
        dst = step if d == 0 else NZ - step
        send(g.at[q, src], g.at[q, dst], ring_s, ring_r.at[d, step - 1, q],
             at_z(1 if d == 0 else -1))

    def ring_here(q, step, d):
        dst = step if d == 0 else NZ - step
        arrived(g.at[q, dst], ring_r.at[d, step - 1, q])

    def in_turn(qs):
        return [pair for q in qs[::2] for pair in ((q, 0), (q + 1, 1), (q + 1, 0), (q, 1))]

    def forward(qs, step):
        for q, d in in_turn(qs):
            if step < 4 or q % 2 == d:
                ring_here(q, step - 1, d)
                ring(q, step, d)

    def here(qs, step):
        for q, d in in_turn(qs):
            ring_here(q, step, d)

    def go(qs, step):
        for q, d in in_turn(qs):
            ring(q, step, d)

    def rest(qs):
        for q, d in in_turn(qs):
            if q % 2 != d:
                ring_here(q, 3, d)

    def last(qs):
        for q in qs:
            ring_here(q, 4, q % 2)

    for q, d in in_turn(range(QN)):
        ring(q, 1, d)
    half = pl.ds(pl.multiple_of(core * (C // 2), C // 2), C // 2)
    other = pl.ds(pl.multiple_of((1 - core) * (C // 2), C // 2), C // 2)
    for j in (2, 1, 3):
        send(w_all.at[0, half], w_all.at[NX - j, half], ws_s, ws_r.at[NX - j - 1], at_x(j))

    hid_in.wait()

    def activate(j):
        x_of = lax.rem(mx + j, NX)

        def body(slot, _):
            r = x_of * NZ + lax.rem(mz - slot + NZ, NZ)
            rows = [hpad[r + i].astype(F32) for i in range(3)]
            out = taps(rows, wpat, 1, False) + down(taps(rows, wpat, 0, False)) + up(taps(rows, wpat, 2, False))
            cs[...] = out
            value = cs[pl.ds(0, W, stride=2), :]
            gate = cs[pl.ds(1, W, stride=2), :]
            sig = 1.0 / (1.0 + jnp.exp(-gate))
            a = gate * sig
            fv[r] = a
            fg[r] = value * sig * (1.0 + gate * (1.0 - sig))
            act = (value * a).astype(BF16)
            if j == 0:
                mix[0, slot] = act
            else:
                mown[j - 1, slot] = act
            return 0

        lax.fori_loop(0, NZ, body, 0)

    def send_mixed(j):
        send(mown.at[j - 1], mix.at[NX - j], mx_s, mx_r.at[NX - j - 1], at_x(j))

    def transposed(j):
        mix_t[j * C:(j + 1) * C, :] = mix[j].reshape(NZ * W, C).T

    groups = ((0, 1, 7), (2, 6), (3, 5), (4,))
    part_of = {slot: n for n, slots in enumerate(groups) for slot in slots}

    def row_of(x_of, slot):
        return x_of * NZ + lax.rem(mz - slot + NZ, NZ)

    def grad_rows(slots):
        total = None
        for q in range(QN):
            left = jnp.concatenate([g[q, s] for s in slots], axis=0)
            right = w_all[:, :, q * QD:(q + 1) * QD].reshape(NX * C, QD)
            part = lax.dot_general(left, right, (((1,), (1,)), ((), ())), preferred_element_type=F32)
            total = part if total is None else total + part
        for n, s in enumerate(slots):
            rows = total[n * W:(n + 1) * W].astype(BF16)
            gmr[row_of(mx, s)] = rows[:, :C]
            for j in range(1, NX):
                gms[j - 1, s] = rows[:, j * C:(j + 1) * C]

    def send_rows(slots):
        for s in slots:
            for j in (2, 1, 3):
                send(gms.at[j - 1, s], gmr.at[row_of(mx, s)], gm_s, gm_r.at[part_of[s]], at_x(j))

    def grad_pre(slots):
        arrived(gms.at[:, pl.ds(0, len(slots))], gm_r.at[part_of[slots[0]]])

        def body(n, sums):
            for s in slots:
                r = row_of(n, s)
                gm = gmr[r].astype(F32)
                gp[r + 1, pl.ds(0, W, stride=2), :] = gm * fv[r]
                gp[r + 1, pl.ds(1, W, stride=2), :] = gm * fg[r]
            for s in slots:
                r = row_of(n, s)
                row = gp[r + 1]
                moved = (up(row), row, down(row))
                new = []
                for i in range(3):
                    hid = hpad[r + i].astype(F32)
                    for j in range(3):
                        prod = (moved[j] * hid).reshape(2 * W // 8, 8, C)
                        new.append(sums[i * 3 + j] + jnp.sum(prod, axis=0))
                sums = tuple(new)
            return sums

        sums = lax.fori_loop(0, NX, body, tuple(cpart[t] for t in range(9)))
        for t in range(9):
            cpart[t] = sums[t]

    def back(slots):
        def body(n, _):
            for s in slots:
                r = row_of(n, s)
                rows = [gp[r + i] for i in range(3)]
                out = taps(rows, wpat, 1, True) + up(taps(rows, wpat, 0, True)) + down(taps(rows, wpat, 2, True))
                ho[r] = out.astype(BF16)
            return 0

        lax.fori_loop(0, NX, body, 0)
        for s in slots:
            for n in range(NX):
                r = row_of(n, s)
                local(ho.at[r], hout_ref.at[r], out_sem)

    def part_dot(q, first, count):
        return jnp.dot(mix_t[:, first * W:(first + count) * W],
                       g[q, first:first + count].reshape(count * W, QD), preferred_element_type=F32)

    def give(u, p1):
        p1s[u] = p1.astype(BF16)
        send(p1s.at[u], p1r.at[u], p1_s, p1_rs.at[u], partner)

    def partial(u):
        give(u, part_dot(2 * u + 1 - core, 0, NZ))
        pacc[u] = part_dot(2 * u + core, 0, NZ)

    def partial_early(u):
        for ref, q in ((p1f, 2 * u + 1 - core), (pacc.at[u], 2 * u + core)):
            ref[...] = part_dot(q, 0, 4) + part_dot(q, 5, 3)

    def partial_late(u):
        give(u, p1f[...] + part_dot(2 * u + 1 - core, 4, 1))
        pacc[u] += part_dot(2 * u + core, 4, 1)

    piece = pl.ds(pl.multiple_of(my * (C // NY), C // NY), C // NY)

    def over_x(u):
        arrived(p1r.at[u], p1_rs.at[u])
        for j in (2, 1, 3, 0):
            rows = slice(j * C, (j + 1) * C)
            s1 = pacc[u, rows] + p1r[u, rows].astype(F32)
            if j == 0:
                pacc[u, rows] = s1
            else:
                r2s[u - 2, j - 1] = s1.astype(BF16)
                send(r2s.at[u - 2, j - 1], r2r.at[u - 2, NX - j - 1], r2_s, r2_rs.at[u - 2], at_x(j))

    def then_y(u):
        s2 = pacc[u, 0:C]
        arrived(r2r.at[u - 2], r2_rs.at[u - 2])
        for j in (1, 3, 2):
            s2 = s2 + r2r[u - 2, j - 1].astype(F32)
        pacc[u, 0:C] = s2
        r3s[u - 2] = s2.astype(BF16).reshape(NY, C // NY, QD)
        for j in far_first:
            send(r3s.at[u - 2, lax.rem(my + j, NY)], r3r.at[u - 2, j - 1], r3_s, r3_rs.at[u - 2], at_y(j))

    def summed_xy(u):
        s3 = pacc[u, piece]
        arrived(r3r.at[u - 2], r3_rs.at[u - 2])
        for j in range(1, NY):
            s3 = s3 + r3r[u - 2, j - 1].astype(F32)
        spread(u, s3)

    def over_y(u):
        arrived(p1r.at[u], p1_rs.at[u])
        for j in range(NX):
            rows = slice(j * C, (j + 1) * C)
            s1 = pacc[u, rows] + p1r[u, rows].astype(F32)
            pacc[u, rows] = s1
            s1 = s1.astype(BF16).reshape(NY, C // NY, QD)
            for y in range(NY):
                ys[u, y, j] = s1[y]
        for j in far_first:
            send(ys.at[u, lax.rem(my + j, NY)], yr.at[u, j - 1], ys_s, ys_r.at[u], at_y(j))

    def then_x(u):
        arrived(yr.at[u], ys_r.at[u])
        for j in (2, 1, 3, 0):
            rows = pl.ds(pl.multiple_of(j * C + my * (C // NY), C // NY), C // NY)
            s2 = pacc[u, rows]
            for n in range(NY - 1):
                s2 = s2 + yr[u, n, j].astype(F32)
            if j == 0:
                pacc[u, rows] = s2
            else:
                xs[u, j - 1] = s2.astype(BF16)
                send(xs.at[u, j - 1], xr.at[u, NX - j - 1], xs_s, xs_r.at[u], at_x(j))

    def summed_yx(u):
        s3 = pacc[u, piece]
        arrived(xr.at[u], xs_r.at[u])
        for j in (1, 3, 2):
            s3 = s3 + xr[u, j - 1].astype(F32)
        spread(u, s3)

    def spread(u, s3):
        pfin[2 * u + core, piece] = (s3 * grad_scale).astype(BF16)
        here = pfin.at[2 * u + core, piece]
        for j in far_first:
            send(here, here, r4_s, r4_rs.at[u], at_y(j))

    def hand_over(u):
        arrived(pfin.at[0, pl.ds(0, C - C // NY)], r4_rs.at[u])
        here = pfin.at[2 * u + core]
        send(here, here, pf_s, pf_r.at[u], partner)
        put(2 * u + core)

    def put(q):
        cols = pl.ds(pl.multiple_of(q * QD, QD), QD)
        local(pfin.at[q], proj_ref.at[:, cols], po_sem)

    def handed(u):
        arrived(pfin.at[2 * u + 1 - core], pf_r.at[u])
        put(2 * u + 1 - core)

    qa, qb, qc = (0, 1, 2, 3), (4, 5), (6, 7)
    for j in (2, 1, 3):
        activate(j)
        send_mixed(j)
    activate(0)
    forward(qa, 2)
    transposed(0)
    for j in (1, 3, 2):
        arrived(w_all.at[j, half], ws_r.at[j - 1])
        send(w_all.at[j, half], w_all.at[j, half], wf_s, wf_r, partner)
    forward(qa, 3)
    forward(qb, 2)
    here(qc, 1)
    arrived(w_all.at[pl.ds(1, NX - 1), other], wf_r)
    grad_rows((0, 1))
    send_rows((0, 1))
    forward(qa, 4)
    grad_rows((7,))
    send_rows((7,))
    for j in (1, 3, 2):
        arrived(mix.at[j], mx_r.at[j - 1])
        transposed(j)
    rest(qa)
    forward(qb, 3)
    go(qc, 2)
    last(qa)
    partial(0)
    forward(qb, 4)
    partial(1)
    over_y(0)
    over_y(1)
    forward(qc, 3)
    rest(qb)
    grad_rows((2, 6))
    send_rows((2, 6))
    last(qb)
    partial(2)
    forward(qc, 4)
    over_x(2)
    rest(qc)
    partial_early(3)
    grad_rows((3, 5))
    last(qc)
    partial_late(3)
    grad_rows((4,))
    over_x(3)
    send_rows((3, 5))
    send_rows((4,))
    grad_pre((0, 1, 7))
    back((0,))
    then_y(2)
    grad_pre((2, 6))
    then_x(0)
    then_x(1)
    back((1, 7))
    then_y(3)
    summed_xy(2)
    grad_pre((3, 5))
    summed_yx(0)
    summed_yx(1)
    grad_pre((4,))
    for t in range(9):
        s = cpart[t]
        cs18[2 * t:2 * t + 2] = (s[0:2] + s[2:4]) + (s[4:6] + s[6:8])
    send(cs18, cr1, c1_s, c1_r, partner)
    back((2, 6))
    summed_xy(3)
    arrived(cr1, c1_r)
    cr2[my] = cs18[...] + cr1[...]
    for j in far_first:
        send(cr2.at[my], cr2.at[my], c2_s, c2_r, at_y(j))
    for u in range(3):
        hand_over(u)
    back((3, 4, 5))
    for u in range(3):
        handed(u)
    hand_over(3)
    arrived(cr2.at[pl.ds(0, NY - 1)], c2_r)
    total = cr2[0]
    for y in range(1, NY):
        total = total + cr2[y]
    for i in range(3):
        for j in range(3):
            t = 2 * (i * 3 + j)
            cg[i, j] = total[t:t + 2] * grad_scale
    cg_out = local(cg, cg_ref, in_sem.at[3])
    handed(3)
    cg_out.wait()
    arrived(ho, out_sem)
    arrived(pfin, po_sem)
    arrived(g.at[:, pl.ds(0, NZ - 1)], ring_s)
    arrived(w_all.at[pl.ds(1, NX - 1), half], ws_s)
    arrived(w_all.at[pl.ds(1, NX - 1), half], wf_s)
    arrived(mown, mx_s)
    arrived(gms, gm_s)
    arrived(p1s, p1_s)
    arrived(r2s, r2_s)
    arrived(r3r, r3_s)
    arrived(yr, ys_s)
    arrived(xs, xs_s)
    arrived(pfin.at[pl.ds(0, QN // 2), pl.ds(0, C - C // NY)], r4_s)
    arrived(pfin.at[pl.ds(0, QN // 2)], pf_s)
    arrived(cs18, c1_s)
    arrived(cr2.at[pl.ds(0, NY - 1)], c2_s)


def deliver(hid_in, proj_in, cg_in, hid_out, proj_out, cg_out, sem):
    moves = [(proj_in, proj_out), (cg_in, cg_out)]
    for n in range(4):
        part = pl.ds(n * (H // 4), H // 4)
        moves.append((hid_in.at[part], hid_out.at[part]))
    copies = [pltpu.make_async_copy(src, dst, sem.at[n]) for n, (src, dst) in enumerate(moves)]
    for copy in copies:
        copy.start()
    for copy in copies:
        copy.wait()


def on_device(hidden_in, conv_weight, proj_weight, out_grad, sample_gate):
    grad_scale = 1.0 / math.sqrt(lax.axis_size("dp") * H * W)
    hbm = pl.BlockSpec(memory_space=pltpu.HBM)
    anywhere = pl.BlockSpec(memory_space=pl.ANY)
    dma = pltpu.SemaphoreType.DMA
    d = proj_weight.shape[1]
    results = (
        jax.ShapeDtypeStruct((H, 2 * W, C), BF16),
        jax.ShapeDtypeStruct((C, d), BF16),
        jax.ShapeDtypeStruct((3, 3, 2, C), F32),
    )
    units, first = QN // 2, 2
    found = pl.pallas_call(
        lambda *refs: kernel(grad_scale, *refs),
        name="mixffn_backward",
        out_shape=results,
        in_specs=[hbm] * 5,
        out_specs=(anywhere,) * 3,
        scratch_shapes=[
            pltpu.VMEM((W, d), BF16),
            pltpu.VMEM((3, 3, 2, C), BF16),
            pltpu.VMEM((1, d), F32),
            pltpu.VMEM((H + 2, 2 * W, C), BF16),
            pltpu.VMEM((9, 8, C), F32),
            pltpu.VMEM((2 * W, C), F32),
            pltpu.VMEM((H, W, C), F32),
            pltpu.VMEM((H, W, C), F32),
            pltpu.VMEM((NX - 1, NZ, W, C), BF16),
            pltpu.VMEM((NX, NZ, W, C), BF16),
            pltpu.VMEM((NX * C, NZ * W), BF16),
            pltpu.VMEM((QN, NZ, W, QD), BF16),
            pltpu.VMEM((NX, C, d), BF16),
            pltpu.VMEM((NX - 1, NZ, W, C), BF16),
            pltpu.VMEM((H, W, C), BF16),
            pltpu.VMEM((H + 2, 2 * W, C), F32),
            pltpu.VMEM((H, 2 * W, C), BF16),
            pltpu.VMEM((units, NX * C, QD), F32),
            pltpu.VMEM((NX * C, QD), F32),
            pltpu.VMEM((units, NX * C, QD), BF16),
            pltpu.VMEM((units, NX * C, QD), BF16),
            pltpu.VMEM((units - first, NX - 1, C, QD), BF16),
            pltpu.VMEM((units - first, NX - 1, C, QD), BF16),
            pltpu.VMEM((units - first, NY, C // NY, QD), BF16),
            pltpu.VMEM((units - first, NY - 1, C // NY, QD), BF16),
            pltpu.VMEM((first, NY, NX, C // NY, QD), BF16),
            pltpu.VMEM((first, NY - 1, NX, C // NY, QD), BF16),
            pltpu.VMEM((first, NX - 1, C // NY, QD), BF16),
            pltpu.VMEM((first, NX - 1, C // NY, QD), BF16),
            pltpu.VMEM((QN, C, QD), BF16),
            pltpu.VMEM((9, 8, C), F32),
            pltpu.VMEM((24, C), F32),
            pltpu.VMEM((24, C), F32),
            pltpu.VMEM((NY, 24, C), F32),
            pltpu.VMEM((3, 3, 2, C), F32),
            dma((6,)), dma, dma,
            dma, dma((2, 4, QN)),
            dma, dma((3,)), dma, dma, dma, dma((3,)),
            dma, dma((4,)),
            dma, dma((units,)), dma, dma((units - first,)), dma, dma((units - first,)),
            dma, dma((first,)), dma, dma((first,)), dma, dma((units,)), dma, dma((units,)),
            dma, dma, dma, dma,
        ],
        compiler_params=pltpu.CompilerParams(
            collective_id=0, has_side_effects=True, vmem_limit_bytes=40 * 1024 * 1024),
    )(*(pltpu.with_memory_space_constraint(a, pltpu.HBM) for a in (
        hidden_in.reshape(H, 2 * W, C),
        conv_weight,
        proj_weight,
        out_grad.reshape(W, d),
        sample_gate,
    )))
    hout, proj, conv = pl.pallas_call(
        deliver,
        name="deliver",
        out_shape=results,
        in_specs=[anywhere] * 3,
        out_specs=(hbm,) * 3,
        scratch_shapes=[dma((6,))],
        compiler_params=pltpu.CompilerParams(vmem_limit_bytes=1024 * 1024),
    )(*found)
    return hout.reshape(hidden_in.shape), proj, conv


def solution(mesh):
    in_specs = (
        P("dp", None, None, None, "tensor"),
        P(None, None, None, "tensor"),
        P("tensor", None),
        P("dp", "tensor", None, None),
        P("dp", None),
    )
    out_specs = (
        P("dp", None, None, None, "tensor"),
        P("tensor", None),
        P(None, None, None, "tensor"),
    )
    return jax.shard_map(
        on_device, mesh=mesh, in_specs=in_specs, out_specs=out_specs, check_vma=False
    )
```

```python
import math

import jax
import jax.numpy as jnp
from jax import lax
from jax.experimental import pallas as pl
from jax.experimental.pallas import tpu as pltpu
from jax.sharding import PartitionSpec as P

NX, NZ, NY = 4, 8, 8
H, W, C = 32, 128, 128
QN, QD = 8, 256
F32, BF16 = jnp.float32, jnp.bfloat16


def down(t):
    rolled = pltpu.roll(t, 2, 0)
    return jnp.where(lax.broadcasted_iota(jnp.int32, t.shape, 0) >= 2, rolled, 0.0)


def up(t):
    n = t.shape[0]
    rolled = pltpu.roll(t, n - 2, 0)
    return jnp.where(lax.broadcasted_iota(jnp.int32, t.shape, 0) < n - 2, rolled, 0.0)


def taps(rows, wpat, j, mirror):
    total = None
    for i in range(3):
        w = wpat[(2 - i if mirror else i) * 3 + j]
        term = rows[i].reshape(2 * W // 8, 8, C) * w[None]
        total = term if total is None else total + term
    return total.reshape(2 * W, C)


def kernel(grad_scale, hid_ref, cw_ref, pw_ref, og_ref, sg_ref, hout_ref, proj_ref, cg_ref,
           og, cw, sg, hpad, wpat, cs, fv, fg, mown, mix, mix_t, g, w_all, gms, gmr, grb, gp, ho,
           pacc, p1f, p1s, p1r, r2s, r2r, r3s, r3r, ys, yr, xs, xr, pfin, cpart, cs18, cr1, cr2, cg,
           met_near, met_far, in_sem, og_sem, out_sem, po_sem, ring_s, ring_r, ws_s, ws_r, wf_s, wf_r, mx_s, mx_r, gm_s, gm_r, gf_s, gr_r,
           p1_s, p1_rs, r2_s, r2_rs, r3_s, r3_rs, ys_s, ys_r, xs_s, xs_r, r4_s, r4_rs, pf_s, pf_r, c1_s, c1_r, c2_s, c2_r):
    dp = lax.axis_index("dp")
    tensor = lax.axis_index("tensor")
    my, core = dp // 2, lax.rem(dp, 2)
    mx, mz = tensor // NZ, lax.rem(tensor, NZ)
    far_first = (4, 3, 5, 2, 6, 1, 7)

    def at_z(d):
        return (dp, mx * NZ + lax.rem(mz + d + NZ, NZ))

    def at_x(j):
        return (dp, lax.rem(mx + j, NX) * NZ + mz)

    def at_y(j):
        return (lax.rem(my + j, NY) * 2 + core, tensor)

    partner = (my * 2 + 1 - core, tensor)

    def send(src, dst, ssem, rsem, to):
        copy = pltpu.make_async_remote_copy(
            src_ref=src, dst_ref=dst, send_sem=ssem, recv_sem=rsem,
            device_id=to, device_id_type=pl.DeviceIdType.MESH)
        copy.start()

    def local(src, dst, sem):
        copy = pltpu.make_async_copy(src, dst, sem)
        copy.start()
        return copy

    def arrived(ref, rsem):
        pltpu.make_async_copy(ref, ref, rsem).wait()

    sg_in = local(sg_ref, sg, in_sem.at[4])
    parts, wide = 4, og.shape[1] // 4
    og_in = [local(og_ref.at[:, pl.ds(n * wide, wide)], og.at[:, pl.ds(n * wide, wide)], og_sem.at[n]) for n in range(parts)]
    barrier = pltpu.get_barrier_semaphore()
    friends = [at_z(1), at_z(-1), partner] + [at_x(j) for j in range(1, NX)] + [at_y(1), at_y(NY - 1)]
    for to in friends:
        pl.semaphore_signal(barrier, inc=1, device_id=to, device_id_type=pl.DeviceIdType.MESH)
    w_in = local(pw_ref, w_all.at[0], in_sem.at[1])
    hid_in = local(hid_ref, hpad.at[pl.ds(1, H)], in_sem.at[2])
    cw_in = local(cw_ref, cw, in_sem.at[5])

    def ring(q, step, d):
        src = step - 1 if d == 0 else (NZ - step + 1) % NZ
        dst = step if d == 0 else NZ - step
        send(g.at[q, src], g.at[q, dst], ring_s, ring_r.at[d, step - 1, q],
             at_z(1 if d == 0 else -1))

    def ring_here(q, step, d):
        dst = step if d == 0 else NZ - step
        arrived(g.at[q, dst], ring_r.at[d, step - 1, q])

    def in_turn(qs):
        return [pair for q in qs[::2] for pair in ((q, 0), (q + 1, 1), (q + 1, 0), (q, 1))]

    def forward(qs, step):
        for q, d in in_turn(qs):
            if step < 4 or q % 2 == d:
                ring_here(q, step - 1, d)
                ring(q, step, d)

    def here(qs, step):
        for q, d in in_turn(qs):
            ring_here(q, step, d)

    def go(qs, step):
        for q, d in in_turn(qs):
            ring(q, step, d)

    def rest(qs):
        for q, d in in_turn(qs):
            if q % 2 != d:
                ring_here(q, 3, d)

    def last(qs):
        for q in qs:
            ring_here(q, 4, q % 2)

    def gated(n):
        og_in[n].wait()
        for q in range(n * QN // parts, (n + 1) * QN // parts):
            cols = slice(q * QD, (q + 1) * QD)
            g[q, 0] = (og[:, cols].astype(F32) * sg[:, cols]).astype(BF16)

    sg_in.wait()
    gated(0)
    pl.semaphore_wait(barrier, len(friends))
    for n in range(parts):
        if n + 1 < parts:
            gated(n + 1)
        go(range(n * QN // parts, (n + 1) * QN // parts), 1)
    w_in.wait()
    for j in (1, NY - 1):
        pl.semaphore_signal(met_near, inc=1, device_id=at_y(j), device_id_type=pl.DeviceIdType.MESH)

    def meet_second():
        pl.semaphore_wait(met_near, 2)
        for j in (2, NY - 2):
            pl.semaphore_signal(met_far, inc=1, device_id=at_y(j), device_id_type=pl.DeviceIdType.MESH)

    def meet_all():
        pl.semaphore_wait(met_far, 2)

    half = pl.ds(pl.multiple_of(core * (C // 2), C // 2), C // 2)
    other = pl.ds(pl.multiple_of((1 - core) * (C // 2), C // 2), C // 2)
    for j in (2, 1, 3):
        send(w_all.at[0, half], w_all.at[NX - j, half], ws_s, ws_r.at[NX - j - 1], at_x(j))

    hpad[0] = jnp.zeros((2 * W, C), BF16)
    hpad[H + 1] = jnp.zeros((2 * W, C), BF16)
    gp[0] = jnp.zeros((2 * W, C), F32)
    gp[H + 1] = jnp.zeros((2 * W, C), F32)
    cs18[...] = jnp.zeros(cs18.shape, F32)
    cpart[...] = jnp.zeros(cpart.shape, F32)
    cw_in.wait()
    even = lax.rem(lax.broadcasted_iota(jnp.int32, (8, C), 0), 2) == 0
    for i in range(3):
        for j in range(3):
            pair = cw[i, j].astype(F32)
            wpat[i * 3 + j] = jnp.where(
                even, jnp.broadcast_to(pair[0:1], (8, C)), jnp.broadcast_to(pair[1:2], (8, C)))
    hid_in.wait()

    def activate(j):
        x_of = lax.rem(mx + j, NX)

        def body(slot, _):
            r = x_of * NZ + lax.rem(mz - slot + NZ, NZ)
            rows = [hpad[r + i].astype(F32) for i in range(3)]
            out = taps(rows, wpat, 1, False) + down(taps(rows, wpat, 0, False)) + up(taps(rows, wpat, 2, False))
            cs[...] = out
            value = cs[pl.ds(0, W, stride=2), :]
            gate = cs[pl.ds(1, W, stride=2), :]
            sig = 1.0 / (1.0 + jnp.exp(-gate))
            a = gate * sig
            fv[r] = a
            fg[r] = value * sig * (1.0 + gate * (1.0 - sig))
            act = (value * a).astype(BF16)
            if j == 0:
                mix[0, slot] = act
            else:
                mown[j - 1, slot] = act
            return 0

        lax.fori_loop(0, NZ, body, 0)

    def send_mixed(j):
        send(mown.at[j - 1], mix.at[NX - j], mx_s, mx_r.at[NX - j - 1], at_x(j))

    def transposed(j):
        mix_t[j * C:(j + 1) * C, :] = mix[j].reshape(NZ * W, C).T

    groups = ((0, 1, 7), (2, 6), (3, 5), (4,))
    part_of = {slot: n for n, slots in enumerate(groups) for slot in slots}

    def row_of(x_of, slot):
        return x_of * NZ + lax.rem(mz - slot + NZ, NZ)

    def grad_rows(slots):
        total = None
        for q in range(QN):
            left = jnp.concatenate([g[q, s] for s in slots], axis=0)
            right = w_all[:, :, q * QD:(q + 1) * QD].reshape(NX * C, QD)
            part = lax.dot_general(left, right, (((1,), (1,)), ((), ())), preferred_element_type=F32)
            total = part if total is None else total + part
        for n, s in enumerate(slots):
            rows = total[n * W:(n + 1) * W].astype(BF16)
            gmr[row_of(mx, s)] = rows[:, :C]
            for j in range(1, NX):
                gms[j - 1, s] = rows[:, j * C:(j + 1) * C]

    way_of = {2: 1, 6: 3}
    spot_of = {2: 0, 6: 1}

    def relay(s):
        way, n = way_of[s], spot_of[s]
        arrived(grb.at[n], gr_r.at[n])
        send(grb.at[n], gmr.at[row_of(lax.rem(mx + NX - way, NX), s)], gf_s, gm_r.at[part_of[s]], at_x(way))

    def send_rows(slots):
        for s in slots:
            if s in way_of:
                send(gms.at[1, s], grb.at[spot_of[s]], gm_s, gr_r.at[spot_of[s]], at_x(way_of[s]))
            for j in (1, 3) if s in way_of else (2, 1, 3):
                send(gms.at[j - 1, s], gmr.at[row_of(mx, s)], gm_s, gm_r.at[part_of[s]], at_x(j))

    def grad_pre(slots):
        arrived(gms.at[:, pl.ds(0, len(slots))], gm_r.at[part_of[slots[0]]])

        def body(n, sums):
            for s in slots:
                r = row_of(n, s)
                gm = gmr[r].astype(F32)
                gp[r + 1, pl.ds(0, W, stride=2), :] = gm * fv[r]
                gp[r + 1, pl.ds(1, W, stride=2), :] = gm * fg[r]
            for s in slots:
                r = row_of(n, s)
                row = gp[r + 1]
                moved = (up(row), row, down(row))
                new = []
                for i in range(3):
                    hid = hpad[r + i].astype(F32)
                    for j in range(3):
                        prod = (moved[j] * hid).reshape(2 * W // 8, 8, C)
                        new.append(sums[i * 3 + j] + jnp.sum(prod, axis=0))
                sums = tuple(new)
            return sums

        sums = lax.fori_loop(0, NX, body, tuple(cpart[t] for t in range(9)))
        for t in range(9):
            cpart[t] = sums[t]

    def back(slots):
        def body(n, _):
            for s in slots:
                r = row_of(n, s)
                rows = [gp[r + i] for i in range(3)]
                out = taps(rows, wpat, 1, True) + up(taps(rows, wpat, 0, True)) + down(taps(rows, wpat, 2, True))
                ho[r] = out.astype(BF16)
            return 0

        lax.fori_loop(0, NX, body, 0)
        for s in slots:
            for n in range(NX):
                r = row_of(n, s)
                local(ho.at[r], hout_ref.at[r], out_sem)

    def part_dot(q, first, count):
        return jnp.dot(mix_t[:, first * W:(first + count) * W],
                       g[q, first:first + count].reshape(count * W, QD), preferred_element_type=F32)

    def give(u, p1):
        p1s[u] = p1.astype(BF16)
        send(p1s.at[u], p1r.at[u], p1_s, p1_rs.at[u], partner)

    def partial(u):
        give(u, part_dot(2 * u + 1 - core, 0, NZ))
        pacc[u] = part_dot(2 * u + core, 0, NZ)

    def partial_early(u):
        for ref, q in ((p1f, 2 * u + 1 - core), (pacc.at[u], 2 * u + core)):
            ref[...] = part_dot(q, 0, 4) + part_dot(q, 5, 3)

    def partial_late(u):
        give(u, p1f[...] + part_dot(2 * u + 1 - core, 4, 1))
        pacc[u] += part_dot(2 * u + core, 4, 1)

    piece = pl.ds(pl.multiple_of(my * (C // NY), C // NY), C // NY)

    by_x, by_y = (0, 2, 3), (1,)

    def over_x(u):
        w = by_x.index(u)
        arrived(p1r.at[u], p1_rs.at[u])
        for j in (2, 1, 3, 0):
            rows = slice(j * C, (j + 1) * C)
            s1 = pacc[u, rows] + p1r[u, rows].astype(F32)
            if j == 0:
                pacc[u, rows] = s1
            else:
                r2s[w, j - 1] = s1.astype(BF16)
                send(r2s.at[w, j - 1], r2r.at[w, NX - j - 1], r2_s, r2_rs.at[w], at_x(j))

    def then_y(u):
        w = by_x.index(u)
        s2 = pacc[u, 0:C]
        arrived(r2r.at[w], r2_rs.at[w])
        for j in (1, 3, 2):
            s2 = s2 + r2r[w, j - 1].astype(F32)
        pacc[u, 0:C] = s2
        r3s[w] = s2.astype(BF16).reshape(NY, C // NY, QD)
        for j in far_first:
            send(r3s.at[w, lax.rem(my + j, NY)], r3r.at[w, j - 1], r3_s, r3_rs.at[w], at_y(j))

    def summed_xy(u):
        w = by_x.index(u)
        s3 = pacc[u, piece]
        arrived(r3r.at[w], r3_rs.at[w])
        for j in range(1, NY):
            s3 = s3 + r3r[w, j - 1].astype(F32)
        spread(u, s3)

    def over_y(u):
        v = by_y.index(u)
        arrived(p1r.at[u], p1_rs.at[u])
        for j in range(NX):
            rows = slice(j * C, (j + 1) * C)
            s1 = pacc[u, rows] + p1r[u, rows].astype(F32)
            pacc[u, rows] = s1
            s1 = s1.astype(BF16).reshape(NY, C // NY, QD)
            for y in range(NY):
                ys[v, y, j] = s1[y]
        for j in far_first:
            send(ys.at[v, lax.rem(my + j, NY)], yr.at[v, j - 1], ys_s, ys_r.at[v], at_y(j))

    def then_x(u):
        v = by_y.index(u)
        arrived(yr.at[v], ys_r.at[v])
        for j in (2, 1, 3, 0):
            rows = pl.ds(pl.multiple_of(j * C + my * (C // NY), C // NY), C // NY)
            s2 = pacc[u, rows]
            for n in range(NY - 1):
                s2 = s2 + yr[v, n, j].astype(F32)
            if j == 0:
                pacc[u, rows] = s2
            else:
                xs[v, j - 1] = s2.astype(BF16)
                send(xs.at[v, j - 1], xr.at[v, NX - j - 1], xs_s, xs_r.at[v], at_x(j))

    def summed_yx(u):
        v = by_y.index(u)
        s3 = pacc[u, piece]
        arrived(xr.at[v], xs_r.at[v])
        for j in (1, 3, 2):
            s3 = s3 + xr[v, j - 1].astype(F32)
        spread(u, s3)

    def spread(u, s3):
        pfin[2 * u + core, piece] = (s3 * grad_scale).astype(BF16)
        here = pfin.at[2 * u + core, piece]
        for j in far_first:
            send(here, here, r4_s, r4_rs.at[u], at_y(j))

    def hand_over(u):
        arrived(pfin.at[0, pl.ds(0, C - C // NY)], r4_rs.at[u])
        here = pfin.at[2 * u + core]
        send(here, here, pf_s, pf_r.at[u], partner)
        put(2 * u + core)

    def put(q):
        cols = pl.ds(pl.multiple_of(q * QD, QD), QD)
        local(pfin.at[q], proj_ref.at[:, cols], po_sem)

    def handed(u):
        arrived(pfin.at[2 * u + 1 - core], pf_r.at[u])
        put(2 * u + 1 - core)

    qa, qb, qc = (0, 1, 2, 3), (4, 5), (6, 7)
    for j in (2, 1, 3):
        activate(j)
        send_mixed(j)
    activate(0)
    forward(qa, 2)
    meet_second()
    transposed(0)
    for j in (1, 3, 2):
        arrived(w_all.at[j, half], ws_r.at[j - 1])
        send(w_all.at[j, half], w_all.at[j, half], wf_s, wf_r, partner)
    forward(qa, 3)
    forward(qb, 2)
    here(qc, 1)
    arrived(w_all.at[pl.ds(1, NX - 1), other], wf_r)
    grad_rows((0, 1))
    send_rows((0, 1))
    meet_all()
    forward(qa, 4)
    grad_rows((7,))
    send_rows((7,))
    for j in (1, 3, 2):
        arrived(mix.at[j], mx_r.at[j - 1])
        transposed(j)
    rest(qa)
    forward(qb, 3)
    go(qc, 2)
    last(qa)
    partial(0)
    forward(qb, 4)
    partial(1)
    over_x(0)
    over_y(1)
    forward(qc, 3)
    rest(qb)
    grad_rows((2, 6))
    send_rows((2, 6))
    last(qb)
    partial(2)
    forward(qc, 4)
    over_x(2)
    rest(qc)
    partial_early(3)
    grad_rows((3, 5))
    relay(2)
    relay(6)
    last(qc)
    partial_late(3)
    grad_rows((4,))
    over_x(3)
    then_x(1)
    then_y(0)
    send_rows((3, 5))
    send_rows((4,))
    grad_pre((0, 1, 7))
    back((0,))
    then_y(2)
    grad_pre((2, 6))
    then_y(3)
    back((1, 7))
    summed_xy(0)
    summed_yx(1)
    summed_xy(2)
    grad_pre((3, 5))
    grad_pre((4,))
    for t in range(9):
        s = cpart[t]
        cs18[2 * t:2 * t + 2] = (s[0:2] + s[2:4]) + (s[4:6] + s[6:8])
    send(cs18, cr1, c1_s, c1_r, partner)
    summed_xy(3)
    back((2,))
    arrived(cr1, c1_r)
    cr2[my] = cs18[...] + cr1[...]
    for j in far_first:
        send(cr2.at[my], cr2.at[my], c2_s, c2_r, at_y(j))
    back((6,))
    back((3, 4, 5))
    for u in range(4):
        hand_over(u)
    for u in range(3):
        handed(u)
    arrived(cr2.at[pl.ds(0, NY - 1)], c2_r)
    total = cr2[0]
    for y in range(1, NY):
        total = total + cr2[y]
    for i in range(3):
        for j in range(3):
            t = 2 * (i * 3 + j)
            cg[i, j] = total[t:t + 2] * grad_scale
    cg_out = local(cg, cg_ref, in_sem.at[3])
    handed(3)
    cg_out.wait()
    arrived(ho, out_sem)
    arrived(pfin, po_sem)
    arrived(g.at[:, pl.ds(0, NZ - 1)], ring_s)
    arrived(w_all.at[pl.ds(1, NX - 1), half], ws_s)
    arrived(w_all.at[pl.ds(1, NX - 1), half], wf_s)
    arrived(mown, mx_s)
    arrived(gms, gm_s)
    arrived(grb, gf_s)
    arrived(p1s, p1_s)
    arrived(r2s, r2_s)
    arrived(r3r, r3_s)
    arrived(yr, ys_s)
    arrived(xs, xs_s)
    arrived(pfin.at[pl.ds(0, QN // 2), pl.ds(0, C - C // NY)], r4_s)
    arrived(pfin.at[pl.ds(0, QN // 2)], pf_s)
    arrived(cs18, c1_s)
    arrived(cr2.at[pl.ds(0, NY - 1)], c2_s)


def deliver(hid_in, proj_in, cg_in, hid_out, proj_out, cg_out, sem):
    moves = [(proj_in, proj_out), (cg_in, cg_out)]
    for n in range(4):
        part = pl.ds(n * (H // 4), H // 4)
        moves.append((hid_in.at[part], hid_out.at[part]))
    copies = [pltpu.make_async_copy(src, dst, sem.at[n]) for n, (src, dst) in enumerate(moves)]
    for copy in copies:
        copy.start()
    for copy in copies:
        copy.wait()


def on_device(hidden_in, conv_weight, proj_weight, out_grad, sample_gate):
    grad_scale = 1.0 / math.sqrt(lax.axis_size("dp") * H * W)
    hbm = pl.BlockSpec(memory_space=pltpu.HBM)
    anywhere = pl.BlockSpec(memory_space=pl.ANY)
    dma = pltpu.SemaphoreType.DMA
    d = proj_weight.shape[1]
    results = (
        jax.ShapeDtypeStruct((H, 2 * W, C), BF16),
        jax.ShapeDtypeStruct((C, d), BF16),
        jax.ShapeDtypeStruct((3, 3, 2, C), F32),
    )
    units, first = QN // 2, 1
    found = pl.pallas_call(
        lambda *refs: kernel(grad_scale, *refs),
        name="mixffn_backward",
        out_shape=results,
        in_specs=[hbm] * 5,
        out_specs=(anywhere,) * 3,
        scratch_shapes=[
            pltpu.VMEM((W, d), BF16),
            pltpu.VMEM((3, 3, 2, C), BF16),
            pltpu.VMEM((1, d), F32),
            pltpu.VMEM((H + 2, 2 * W, C), BF16),
            pltpu.VMEM((9, 8, C), F32),
            pltpu.VMEM((2 * W, C), F32),
            pltpu.VMEM((H, W, C), F32),
            pltpu.VMEM((H, W, C), F32),
            pltpu.VMEM((NX - 1, NZ, W, C), BF16),
            pltpu.VMEM((NX, NZ, W, C), BF16),
            pltpu.VMEM((NX * C, NZ * W), BF16),
            pltpu.VMEM((QN, NZ, W, QD), BF16),
            pltpu.VMEM((NX, C, d), BF16),
            pltpu.VMEM((NX - 1, NZ, W, C), BF16),
            pltpu.VMEM((H, W, C), BF16),
            pltpu.VMEM((2, W, C), BF16),
            pltpu.VMEM((H + 2, 2 * W, C), F32),
            pltpu.VMEM((H, 2 * W, C), BF16),
            pltpu.VMEM((units, NX * C, QD), F32),
            pltpu.VMEM((NX * C, QD), F32),
            pltpu.VMEM((units, NX * C, QD), BF16),
            pltpu.VMEM((units, NX * C, QD), BF16),
            pltpu.VMEM((units - first, NX - 1, C, QD), BF16),
            pltpu.VMEM((units - first, NX - 1, C, QD), BF16),
            pltpu.VMEM((units - first, NY, C // NY, QD), BF16),
            pltpu.VMEM((units - first, NY - 1, C // NY, QD), BF16),
            pltpu.VMEM((first, NY, NX, C // NY, QD), BF16),
            pltpu.VMEM((first, NY - 1, NX, C // NY, QD), BF16),
            pltpu.VMEM((first, NX - 1, C // NY, QD), BF16),
            pltpu.VMEM((first, NX - 1, C // NY, QD), BF16),
            pltpu.VMEM((QN, C, QD), BF16),
            pltpu.VMEM((9, 8, C), F32),
            pltpu.VMEM((24, C), F32),
            pltpu.VMEM((24, C), F32),
            pltpu.VMEM((NY, 24, C), F32),
            pltpu.VMEM((3, 3, 2, C), F32),
            pltpu.SemaphoreType.REGULAR, pltpu.SemaphoreType.REGULAR,
            dma((6,)), dma((4,)), dma, dma,
            dma, dma((2, 4, QN)),
            dma, dma((3,)), dma, dma, dma, dma((3,)),
            dma, dma((4,)), dma, dma((2,)),
            dma, dma((units,)), dma, dma((units - first,)), dma, dma((units - first,)),
            dma, dma((first,)), dma, dma((first,)), dma, dma((units,)), dma, dma((units,)),
            dma, dma, dma, dma,
        ],
        compiler_params=pltpu.CompilerParams(
            collective_id=0, has_side_effects=True, vmem_limit_bytes=40 * 1024 * 1024),
    )(*(pltpu.with_memory_space_constraint(a, pltpu.HBM) for a in (
        hidden_in.reshape(H, 2 * W, C),
        conv_weight,
        proj_weight,
        out_grad.reshape(W, d),
        sample_gate,
    )))
    hout, proj, conv = pl.pallas_call(
        deliver,
        name="deliver",
        out_shape=results,
        in_specs=[anywhere] * 3,
        out_specs=(hbm,) * 3,
        scratch_shapes=[dma((6,))],
        compiler_params=pltpu.CompilerParams(vmem_limit_bytes=1024 * 1024),
    )(*found)
    return hout.reshape(hidden_in.shape), proj, conv


def solution(mesh):
    in_specs = (
        P("dp", None, None, None, "tensor"),
        P(None, None, None, "tensor"),
        P("tensor", None),
        P("dp", "tensor", None, None),
        P("dp", None),
    )
    out_specs = (
        P("dp", None, None, None, "tensor"),
        P("tensor", None),
        P(None, None, None, "tensor"),
    )
    return jax.shard_map(
        on_device, mesh=mesh, in_specs=in_specs, out_specs=out_specs, check_vma=False
    )
```
